512 devices in a mesh: row: 16 (over z), col: 32 (over y, x, core).
Axes of the slice: x: 4, y: 4, z: 16, core: 2. Of those that a mesh axis runs over, the one named last changes fastest.
Arguments:
- covariance: float32 [16384, 16384], P('row', 'col'), as said below
- fields: float32 [512, 16384], P('col', 'row'), may hold values from -6 to 6
Outputs:
- factored: float32 [16384, 16384], P('row', 'col')
- solved_fields: float32 [512, 16384], P('col', 'row')
The draws below stay inside these ranges and needn't reach their ends.
Inputs may be any that keep to these rules, and one draw needn't show every extreme that they name: covariance, read in the global order of the steps, is symmetric positive definite.
All inputs are finite; a program needn't handle non-finite values.
Results may differ from the reference program's by a relative error of at most 0.0003.
Values sent between devices are 32-bit elements; how exact they have to be, the bound alone decides.
No kernel may reach another device: no remote copies, remote signals or barrier semaphores. Data moves between devices by JAX's collectives and lax.ppermute only.
A program may use at most 64 MiB of HBM per device.

```python
import math
import jax
import jax.numpy as jnp
from jax import lax

ORDER = 16384
NB = 512
FIELDS = 512
ROWS_DEV = 1024
COLS_DEV = 512
BLOCK = 16
N_ROW = 16
N_COL = 32


NUGGET = 0.3


RANGE = 0.1


def stored_to_global(count, block, groups):
    stored = jnp.arange(count, dtype=jnp.int32)
    share = count // groups
    return (stored % share // block * groups + stored // share) * block + stored % block


def draw_covariance(key, part):
    block = NB // N_COL
    points = jax.random.uniform(jax.random.fold_in(key, 11), (ORDER, 2), jnp.float32)
    rows_global = stored_to_global(ORDER, block, N_ROW)
    cols_global = stored_to_global(ORDER, block, N_COL)
    col_points = points[cols_global]
    stretch = math.sqrt(3.0) / RANGE
    height = math.gcd(ORDER, 1024)

    def one_block(row_ids):
        row_points = points[row_ids]
        delta_x = row_points[:, 0:1] - col_points[None, :, 0]
        delta_y = row_points[:, 1:2] - col_points[None, :, 1]
        scaled = jnp.sqrt(delta_x * delta_x + delta_y * delta_y) * stretch
        kernel = (1.0 + scaled) * jnp.exp(-scaled)
        kernel = kernel + jnp.where(row_ids[:, None] == cols_global[None, :], NUGGET, 0.0)
        return kernel
    blocks = lax.map(one_block, rows_global.reshape(ORDER // height, height))
    return blocks.reshape(ORDER, ORDER).astype(jnp.float32)


def levels(own_key, shape, cuts, smallest, high):
    def one(position, parts):
        heights = jax.random.uniform(jax.random.fold_in(jax.random.fold_in(own_key, 6), position), (parts,), jnp.float32, smallest / len(cuts), high / len(cuts))
        return jnp.repeat(jnp.exp(heights), shape[position] // parts).reshape((-1,) + (1,) * (len(shape) - position - 1))

    factor_of = one(*cuts[0])
    for cut in cuts[1:]:
        factor_of = factor_of * one(*cut)
    return factor_of


def normal_values(key, extent, scale, most, shards=(), held_as=jnp.bfloat16):
    values = scale * jax.random.normal(key, extent, jnp.float32)
    if shards:
        values = values * levels(key, extent, shards, -0.22, 0.18)
    return jnp.clip(values, -most, most).astype(held_as)


def setup_inputs(seed: int = 0) -> dict:
    streams_of = jax.random.split(jax.random.key(seed), 3)
    return {
        "covariance": draw_covariance(jax.random.fold_in(streams_of[2], 71), 0),
        "fields": normal_values(streams_of[1], (FIELDS, ORDER), 1.0, 6.0, ((0, 32), (1, 16)), jnp.float32),
    }


PRECISE = lax.Precision.HIGHEST

def reference(covariance, fields):
    matrix = covariance.reshape(N_ROW, ROWS_DEV // BLOCK, BLOCK, N_COL, COLS_DEV // BLOCK, BLOCK)
    matrix = matrix.transpose(1, 0, 2, 4, 3, 5).reshape(ORDER, ORDER)
    field_rows = fields.reshape(FIELDS, N_ROW, ROWS_DEV // BLOCK, BLOCK).transpose(0, 2, 1, 3).reshape(FIELDS, ORDER)
    positions = jnp.arange(ORDER, dtype=jnp.int32)[:, None]
    panels = []
    for step in range(2):
        lower = step * NB
        higher = lower + NB
        factor = jnp.linalg.cholesky(matrix[lower:higher, lower:higher])
        inverse = jax.scipy.linalg.solve_triangular(factor, jnp.eye(NB, dtype=matrix.dtype), lower=True)
        product = jnp.dot(matrix[:, lower:higher], inverse.T, precision=PRECISE)
        column = jnp.where(positions < lower, 0.0, product).at[lower:higher].set(factor)
        trail = jnp.where(positions >= higher, column, 0.0)
        solved = jnp.dot(field_rows[:, lower:higher], inverse.T, precision=PRECISE)
        field_rows = (field_rows - jnp.dot(solved, trail.T, precision=PRECISE)).at[:, lower:higher].set(solved)
        matrix = matrix.at[:, higher:].add(-jnp.dot(trail, trail[higher:].T, precision=PRECISE))
        panels.append(column)
    remainder = jnp.where(positions < 2 * NB, 0.0, matrix[:, 2 * NB:])
    matrix = jnp.concatenate([panels[0], panels[1], remainder], axis=1)
    matrix = matrix.reshape(ROWS_DEV // BLOCK, N_ROW, BLOCK, COLS_DEV // BLOCK, N_COL, BLOCK)
    factored = matrix.transpose(1, 0, 2, 4, 3, 5).reshape(ORDER, ORDER)
    solved_fields = field_rows.reshape(FIELDS, ROWS_DEV // BLOCK, N_ROW, BLOCK).transpose(0, 2, 1, 3).reshape(FIELDS, ORDER)
    return (factored, solved_fields)
```

```python
import functools

import jax
import jax.numpy as jnp
from jax import lax
from jax.experimental import pallas as pl
from jax.experimental.pallas import tpu as pltpu
from jax.sharding import PartitionSpec as P

F32 = jnp.float32
BF16 = jnp.bfloat16
HI = lax.Precision.HIGHEST
NB = 512
WIDE = 2 * NB


def mm(a, b):
    return lax.dot_general(a, b, (((1,), (0,)), ((), ())), precision=HI, preferred_element_type=F32)

def tmm(a, b):
    return lax.dot_general(a, b, (((0,), (0,)), ((), ())), precision=HI, preferred_element_type=F32)

def eliminate(t, out_ref, rows=32, size=128):
    lane = lax.broadcasted_iota(jnp.int32, (8, size), 1)
    sub = lax.broadcasted_iota(jnp.int32, (8, size), 0)
    nv = rows // 8
    for p in range(size // rows):
        k0 = p * rows
        R = [t[8 * v:8 * v + 8, :] for v in range(nv)]
        for s in range(nv):
            c0 = k0 + 8 * s
            inside = (lane >= c0) & (lane < c0 + 8)
            B = [[None] * nv for _ in range(8)]
            for j in range(8):
                for v in range(s, nv):
                    B[j][v] = jnp.broadcast_to(R[v][:, c0 + j:c0 + j + 1], (8, size))
            R[s] = jnp.where(inside, jnp.where(lane - c0 == sub, 1.0, 0.0), R[s])
            for v in range(s + 1, nv):
                R[v] = jnp.where(inside, 0.0, R[v])
            scale = jnp.zeros((8, size), F32)
            for j in range(8):
                d = jnp.broadcast_to(B[j][s][j:j + 1, :], (8, size))
                scale = jnp.where(sub == j, d, scale)
                inv = 1.0 / d
                bl = [None] * 8
                for l in range(j + 1, 8):
                    bl[l] = jnp.broadcast_to(B[l][s][j:j + 1, :], (8, size))
                r = jnp.broadcast_to(R[s][j:j + 1, :], (8, size))
                for v in range(s, nv):
                    m = B[j][v] * inv
                    if v == s:
                        m = jnp.where(sub > j, m, 0.0)
                    for l in range(j + 1, 8):
                        B[l][v] = B[l][v] - m * bl[l]
                    R[v] = R[v] - m * r
            R[s] = R[s] * (1.0 / jnp.sqrt(scale))
        panel = jnp.concatenate(R, axis=0) if nv > 1 else R[0]
        out_ref[k0:k0 + rows, :] = panel
        k1 = k0 + rows
        if k1 < size:
            lane_r = lax.broadcasted_iota(jnp.int32, (rows, size), 1)
            rest = t[rows:, :]
            lr = lax.broadcasted_iota(jnp.int32, rest.shape, 1)
            rest = jnp.where((lr >= k0) & (lr < k1), 0.0, rest)
            sub_r = lax.broadcasted_iota(jnp.int32, (rows, size), 0)
            right = jnp.where((lane_r < k1) & (lane_r - k0 > sub_r), 0.0, panel)
            up = tmm(panel, right)
            t = rest - up[k1:, :]

def factor_kernel(at_ref, own_ref, other_ref, w_ref, w2, rbuf, blk):
    nb = 256
    steps = WIDE // nb
    chips, block, _ = own_ref.shape
    core = at_ref[1] % 2
    for ref, side in ((own_ref, core), (other_ref, 1 - core)):
        for c in range(chips):
            lo = pl.multiple_of((2 * c + side) * block, block)
            w_ref[pl.ds(lo, block), :] = ref[c, :, 0:WIDE]
            w_ref[pl.ds(NB + lo, block), NB:WIDE] = ref[c, :, WIDE : WIDE + NB]
    w_ref[NB:WIDE, 0:NB] = jnp.zeros((NB, NB), F32)
    tri = (lax.broadcasted_iota(jnp.int32, (128, 128), 0) >= lax.broadcasted_iota(jnp.int32, (128, 128), 1))

    def outer(k, _):
        o = pl.multiple_of(k * nb, nb)
        oa, ob = pl.ds(o, 128), pl.ds(pl.multiple_of(o + 128, 128), 128)
        eliminate(w_ref[oa, oa], blk)
        waa = jnp.where(tri, blk[...], 0.0)
        w2[0:128, 0:128] = waa
        w2[0:128, 128:256] = jnp.zeros((128, 128), F32)
        uab = mm(waa, w_ref[oa, ob])
        vba = -tmm(uab, waa)
        eliminate(w_ref[ob, ob] - tmm(uab, uab), blk)
        wbb = jnp.where(tri, blk[...], 0.0)
        w2[128:256, 128:256] = wbb
        w2[128:256, 0:128] = mm(wbb, vba)
        row = pl.ds(o, nb)

        def scale(c, _):
            col = pl.ds(pl.multiple_of(c * nb, nb), nb)

            @pl.when(c != k)
            def _():
                rbuf[:, col] = mm(w2[...], w_ref[row, col])

            @pl.when(c == k)
            def _():
                rbuf[:, col] = w2[...]

            @pl.when(c <= k)
            def _():
                w_ref[row, col] = rbuf[:, col]

            @pl.when(c > k)
            def _():
                w_ref[row, col] = jnp.zeros((nb, nb), F32)
            return 0

        lax.fori_loop(0, steps, scale, 0)

        def below(j, _):
            jo = pl.ds(pl.multiple_of(j * nb, nb), nb)

            def one(c, _):
                col = pl.ds(pl.multiple_of(c * nb, nb), nb)

                @pl.when((c < k) | (c >= j))
                def _():
                    w_ref[jo, col] = w_ref[jo, col] - tmm(rbuf[:, jo], rbuf[:, col])

                @pl.when(c == k)
                def _():
                    w_ref[jo, col] = -tmm(rbuf[:, jo], rbuf[:, col])
                return 0

            lax.fori_loop(0, steps, one, 0)
            return 0

        lax.fori_loop(k + 1, steps, below, 0)
        return 0

    lax.fori_loop(0, steps, outer, 0)

def inverse_factor(at, own, other):
    vmem = pl.BlockSpec(memory_space=pltpu.VMEM)
    return pl.pallas_call(
        factor_kernel,
        out_shape=jax.ShapeDtypeStruct((WIDE, WIDE), F32),
        in_specs=[pl.BlockSpec(memory_space=pltpu.SMEM), vmem, vmem],
        out_specs=vmem,
        scratch_shapes=[pltpu.VMEM((256, 256), F32), pltpu.VMEM((256, WIDE), F32), pltpu.VMEM((128, 128), F32)],
        compiler_params=pltpu.CompilerParams(vmem_limit_bytes=24 << 20),
        cost_estimate=pl.CostEstimate(flops=8_000_000_000, bytes_accessed=8 << 20, transcendentals=0),
        name="inverse_factor",
    )(at, own, other)


def split(x):
    high = x.astype(BF16)
    return high, (x - high.astype(F32)).astype(BF16)


def column_kernel(w_ref, g_ref, high_ref, low_ref, y_ref, a_ref):
    groups, top, wide = g_ref.shape
    block = 16
    size = groups * block
    for q in range(top // block):
        a_ref[q * size : (q + 1) * size, :] = g_ref[:, q * block : (q + 1) * block, :].reshape(size, wide)
    for i in range(0, WIDE, size):
        z = mm(w_ref[i : i + size, : i + size], a_ref[: i + size, :])
        high_ref[i : i + size, :], low_ref[i : i + size, :] = split(z)
        y_ref[i : i + size, :] = z[:, wide - 128 :]


def column_part(w, gathered):
    vmem = pl.BlockSpec(memory_space=pltpu.VMEM)
    wide = gathered.shape[2]
    return pl.pallas_call(
        column_kernel,
        out_shape=(
            jax.ShapeDtypeStruct((WIDE, wide), BF16),
            jax.ShapeDtypeStruct((WIDE, wide), BF16),
            jax.ShapeDtypeStruct((WIDE, 128), F32),
        ),
        in_specs=[vmem, vmem],
        out_specs=(vmem, vmem, vmem),
        scratch_shapes=[pltpu.VMEM((WIDE, wide), F32)],
        compiler_params=pltpu.CompilerParams(vmem_limit_bytes=24 << 20),
        cost_estimate=pl.CostEstimate(flops=6_000_000_000, bytes_accessed=8 << 20, transcendentals=0),
        name="column_part",
    )(w, gathered)


def row_kernel(at_ref, w_ref, high_ref, low_ref, g_ref, cov_ref, field_ref, out_ref, fout_ref, p_ref, x_ref):
    column_groups, _, block, tile = g_ref.shape
    row_groups = 16
    columns = cov_ref.shape[1]
    width = field_ref.shape[0]
    size = 256
    own = 2 * block
    for p in range(2):
        p_ref[p * NB : (p + 1) * NB, :] = g_ref[:, p].reshape(NB, tile)
    for i in range(0, WIDE, size):
        x_ref[i : i + size, :] = mm(w_ref[i : i + size, : i + size], p_ref[: i + size, :])
    x_high, x_low = split(x_ref[...].T)
    z_high, z_low = high_ref[...], low_ref[...]

    def dot(a, b):
        return jnp.dot(a, b, preferred_element_type=F32)

    change = dot(x_high, z_high) + (dot(x_high, z_low) + dot(x_low, z_high))
    local = lax.broadcasted_iota(jnp.int32, (tile, 1), 0) + pl.program_id(0) * tile
    rows = (local // block * row_groups + at_ref[0]) * block + local % block
    mine = pl.multiple_of(at_ref[1] * block, block)
    edge = jnp.concatenate([x_ref[pl.ds(mine, block), :], x_ref[pl.ds(NB + mine, block), :]], axis=0).T
    lane = lax.broadcasted_iota(jnp.int32, (1, own), 1)
    lanes = (lane // block * column_groups + at_ref[1]) * block + lane % block
    out_ref[...] = jnp.where(rows < WIDE, 0.0, cov_ref[...] - change[:, :columns])
    out_ref[:, :own] = jnp.where(rows >= lanes, edge, 0.0)
    fout_ref[...] = field_ref[...] - change[:, columns:].T[:width]


def row_part(at, w, high, low, gathered, covariance, fields):
    vmem = pl.BlockSpec(memory_space=pltpu.VMEM)
    tile = 256
    groups, _, block, local_rows = gathered.shape
    columns = covariance.shape[1]
    width = fields.shape[0]
    return pl.pallas_call(
        row_kernel,
        grid=(local_rows // tile,),
        out_shape=(
            jax.ShapeDtypeStruct(covariance.shape, F32),
            jax.ShapeDtypeStruct(fields.shape, F32),
        ),
        in_specs=[
            pl.BlockSpec(memory_space=pltpu.SMEM),
            vmem,
            vmem,
            vmem,
            pl.BlockSpec((groups, 2, block, tile), lambda i: (0, 0, 0, i)),
            pl.BlockSpec((tile, columns), lambda i: (i, 0)),
            pl.BlockSpec((width, tile), lambda i: (0, i)),
        ],
        out_specs=(
            pl.BlockSpec((tile, columns), lambda i: (i, 0)),
            pl.BlockSpec((width, tile), lambda i: (0, i)),
        ),
        scratch_shapes=[pltpu.VMEM((WIDE, tile), F32), pltpu.VMEM((WIDE, tile), F32)],
        compiler_params=pltpu.CompilerParams(vmem_limit_bytes=40 << 20),
        cost_estimate=pl.CostEstimate(flops=12_000_000_000, bytes_accessed=16 << 20, transcendentals=0),
        name="row_part",
    )(at, w, high, low, gathered, covariance, fields)


def spread_out(piece, axis, count, groups=None):
    copies = jnp.broadcast_to(piece[None], (count,) + piece.shape)
    return lax.all_to_all(copies, axis, 0, 0, axis_index_groups=groups, tiled=True)


def finish(at, covariance, fields, own_pieces, other_pieces, panel, across):
    width = fields.shape[0]
    w = inverse_factor(at, own_pieces, other_pieces)
    high, low, y = column_part(w, across)
    factored, moved = row_part(at, w, high, low, panel, covariance, fields)
    row_groups, top, _ = across.shape
    block = WIDE // row_groups // (top // 16)
    solved = y.reshape(top // block, row_groups, block, 128)
    solved = lax.dynamic_index_in_dim(solved, at[0], 1, keepdims=False).reshape(top, 128)[:, :width]
    return (factored, moved.at[:, :top].set(solved.T))


def shards(covariance, fields):
    rows_n = lax.axis_size("row")
    cols_n = lax.axis_size("col")
    at = jnp.stack([lax.axis_index("row"), lax.axis_index("col")]).astype(jnp.int32)
    local_rows, local_columns = covariance.shape
    width = fields.shape[0]
    block = NB // cols_n
    top = WIDE // rows_n
    own = 2 * block
    quarters = top // block
    cores = 2

    corner = covariance[:top, :own]
    packed = jnp.concatenate([corner[q * block : (q + 1) * block] for q in range(quarters)], axis=1)
    tall = spread_out(packed, "row", rows_n).reshape(rows_n * block, quarters * own).T
    strip = jnp.concatenate([tall[q * own : (q + 1) * own] for q in range(quarters)], axis=1)
    strip = jnp.concatenate([strip[:block], strip[block:, NB:]], axis=1)
    same_core = [[cores * i + k for i in range(cols_n // cores)] for k in range(cores)]
    own_pieces = spread_out(strip, "col", cols_n // cores, same_core)
    other_pieces = lax.ppermute(own_pieces, "col", [(i, i ^ 1) for i in range(cols_n)])

    across = jnp.concatenate([covariance[:top], jnp.pad(fields[:, :top].T, ((0, 0), (0, 128 - width)))], axis=1)
    across = lax.all_gather(across, "row", axis=0)
    panel = covariance[:, :own].T.reshape(2, block, local_rows)
    panel = lax.all_gather(panel, "col", axis=0)
    return finish(at, covariance, fields, own_pieces, other_pieces, panel, across)


def solution(mesh):
    return jax.shard_map(
        shards,
        mesh=mesh,
        in_specs=(P("row", "col"), P("col", "row")),
        out_specs=(P("row", "col"), P("col", "row")),
        check_vma=False,
    )
```

```python
import functools

import jax
import jax.numpy as jnp
from jax import lax
from jax.experimental import pallas as pl
from jax.experimental.pallas import tpu as pltpu
from jax.sharding import PartitionSpec as P

F32 = jnp.float32
BF16 = jnp.bfloat16
HI = lax.Precision.HIGHEST
NB = 512
WIDE = 2 * NB


def mm(a, b):
    return lax.dot_general(a, b, (((1,), (0,)), ((), ())), precision=HI, preferred_element_type=F32)

def tmm(a, b):
    return lax.dot_general(a, b, (((0,), (0,)), ((), ())), precision=HI, preferred_element_type=F32)

def eliminate(t, out_ref, rows=32, size=128):
    lane = lax.broadcasted_iota(jnp.int32, (8, size), 1)
    sub = lax.broadcasted_iota(jnp.int32, (8, size), 0)
    nv = rows // 8
    for p in range(size // rows):
        k0 = p * rows
        R = [t[8 * v:8 * v + 8, :] for v in range(nv)]
        for s in range(nv):
            c0 = k0 + 8 * s
            inside = (lane >= c0) & (lane < c0 + 8)
            B = [[None] * nv for _ in range(8)]
            for j in range(8):
                for v in range(s, nv):
                    B[j][v] = jnp.broadcast_to(R[v][:, c0 + j:c0 + j + 1], (8, size))
            R[s] = jnp.where(inside, jnp.where(lane - c0 == sub, 1.0, 0.0), R[s])
            for v in range(s + 1, nv):
                R[v] = jnp.where(inside, 0.0, R[v])
            scale = jnp.zeros((8, size), F32)
            for j in range(8):
                d = jnp.broadcast_to(B[j][s][j:j + 1, :], (8, size))
                scale = jnp.where(sub == j, d, scale)
                inv = 1.0 / d
                bl = [None] * 8
                for l in range(j + 1, 8):
                    bl[l] = jnp.broadcast_to(B[l][s][j:j + 1, :], (8, size))
                r = jnp.broadcast_to(R[s][j:j + 1, :], (8, size))
                for v in range(s, nv):
                    m = B[j][v] * inv
                    if v == s:
                        m = jnp.where(sub > j, m, 0.0)
                    for l in range(j + 1, 8):
                        B[l][v] = B[l][v] - m * bl[l]
                    R[v] = R[v] - m * r
            R[s] = R[s] * (1.0 / jnp.sqrt(scale))
        panel = jnp.concatenate(R, axis=0) if nv > 1 else R[0]
        out_ref[k0:k0 + rows, :] = panel
        k1 = k0 + rows
        if k1 < size:
            lane_r = lax.broadcasted_iota(jnp.int32, (rows, size), 1)
            rest = t[rows:, :]
            lr = lax.broadcasted_iota(jnp.int32, rest.shape, 1)
            rest = jnp.where((lr >= k0) & (lr < k1), 0.0, rest)
            sub_r = lax.broadcasted_iota(jnp.int32, (rows, size), 0)
            right = jnp.where((lane_r < k1) & (lane_r - k0 > sub_r), 0.0, panel)
            up = tmm(panel, right)
            t = rest - up[k1:, :]

def factor_kernel(at_ref, own_ref, other_ref, w_ref, w2, rbuf, blk):
    nb = 256
    steps = WIDE // nb
    chips, block, _ = own_ref.shape
    core = at_ref[1] % 2
    for ref, side in ((own_ref, core), (other_ref, 1 - core)):
        for c in range(chips):
            lo = pl.multiple_of((2 * c + side) * block, block)
            w_ref[pl.ds(lo, block), :] = ref[c, :, 0:WIDE]
            w_ref[pl.ds(NB + lo, block), NB:WIDE] = ref[c, :, WIDE : WIDE + NB]
    w_ref[NB:WIDE, 0:NB] = jnp.zeros((NB, NB), F32)
    tri = (lax.broadcasted_iota(jnp.int32, (128, 128), 0) >= lax.broadcasted_iota(jnp.int32, (128, 128), 1))

    def outer(k, _):
        o = pl.multiple_of(k * nb, nb)
        oa, ob = pl.ds(o, 128), pl.ds(pl.multiple_of(o + 128, 128), 128)
        eliminate(w_ref[oa, oa], blk)
        waa = jnp.where(tri, blk[...], 0.0)
        w2[0:128, 0:128] = waa
        w2[0:128, 128:256] = jnp.zeros((128, 128), F32)
        uab = mm(waa, w_ref[oa, ob])
        vba = -tmm(uab, waa)
        eliminate(w_ref[ob, ob] - tmm(uab, uab), blk)
        wbb = jnp.where(tri, blk[...], 0.0)
        w2[128:256, 128:256] = wbb
        w2[128:256, 0:128] = mm(wbb, vba)
        row = pl.ds(o, nb)

        def scale(c, _):
            col = pl.ds(pl.multiple_of(c * nb, nb), nb)

            @pl.when(c != k)
            def _():
                rbuf[:, col] = mm(w2[...], w_ref[row, col])

            @pl.when(c == k)
            def _():
                rbuf[:, col] = w2[...]

            @pl.when(c <= k)
            def _():
                w_ref[row, col] = rbuf[:, col]

            @pl.when(c > k)
            def _():
                w_ref[row, col] = jnp.zeros((nb, nb), F32)
            return 0

        lax.fori_loop(0, steps, scale, 0)

        def below(j, _):
            jo = pl.ds(pl.multiple_of(j * nb, nb), nb)

            def one(c, _):
                col = pl.ds(pl.multiple_of(c * nb, nb), nb)

                @pl.when((c < k) | (c >= j))
                def _():
                    w_ref[jo, col] = w_ref[jo, col] - tmm(rbuf[:, jo], rbuf[:, col])

                @pl.when(c == k)
                def _():
                    w_ref[jo, col] = -tmm(rbuf[:, jo], rbuf[:, col])
                return 0

            lax.fori_loop(0, steps, one, 0)
            return 0

        lax.fori_loop(k + 1, steps, below, 0)
        return 0

    lax.fori_loop(0, steps, outer, 0)

def inverse_factor(at, own, other):
    vmem = pl.BlockSpec(memory_space=pltpu.VMEM)
    return pl.pallas_call(
        factor_kernel,
        out_shape=jax.ShapeDtypeStruct((WIDE, WIDE), F32),
        in_specs=[pl.BlockSpec(memory_space=pltpu.SMEM), vmem, vmem],
        out_specs=vmem,
        scratch_shapes=[pltpu.VMEM((256, 256), F32), pltpu.VMEM((256, WIDE), F32), pltpu.VMEM((128, 128), F32)],
        compiler_params=pltpu.CompilerParams(vmem_limit_bytes=12 << 20),
        cost_estimate=pl.CostEstimate(flops=8_000_000_000, bytes_accessed=8 << 20, transcendentals=0),
        name="inverse_factor",
    )(at, own, other)


def split(x):
    high = x.astype(BF16)
    return high, (x - high.astype(F32)).astype(BF16)


def panel_kernel(at_ref, w_ref, own_ref, other_ref, high_ref, low_ref, edge_ref, p_ref, x_ref):
    chips, _, block, tile = own_ref.shape
    column_groups, row_groups = 2 * chips, 16
    size = 256
    core = at_ref[1] % 2
    for ref, side in ((own_ref, core), (other_ref, 1 - core)):
        for c in range(chips):
            for p in range(2):
                lo = pl.multiple_of(p * NB + (2 * c + side) * block, block)
                p_ref[pl.ds(lo, block), :] = ref[c, p]
    for i in range(0, WIDE, size):
        x = mm(w_ref[i : i + size, : i + size], p_ref[: i + size, :])
        x_ref[i : i + size, :] = x
        high_ref[:, i : i + size], low_ref[:, i : i + size] = split(x.T)
    mine = pl.multiple_of(at_ref[1] * block, block)
    edge = jnp.concatenate([x_ref[pl.ds(mine, block), :], x_ref[pl.ds(NB + mine, block), :]], axis=0).T
    local = lax.broadcasted_iota(jnp.int32, (tile, 1), 0) + pl.program_id(0) * tile
    rows = (local // block * row_groups + at_ref[0]) * block + local % block
    lane = lax.broadcasted_iota(jnp.int32, (1, 2 * block), 1)
    lanes = (lane // block * column_groups + at_ref[1]) * block + lane % block
    edge_ref[:, : 2 * block] = jnp.where(rows >= lanes, edge, 0.0)


def panel_part(at, w, own, other):
    vmem = pl.BlockSpec(memory_space=pltpu.VMEM)
    tile = 256
    chips, _, block, local_rows = own.shape
    halves = pl.BlockSpec((chips, 2, block, tile), lambda i: (0, 0, 0, i))
    return pl.pallas_call(
        panel_kernel,
        grid=(local_rows // tile,),
        out_shape=(
            jax.ShapeDtypeStruct((local_rows, WIDE), BF16),
            jax.ShapeDtypeStruct((local_rows, WIDE), BF16),
            jax.ShapeDtypeStruct((local_rows, 128), F32),
        ),
        in_specs=[pl.BlockSpec(memory_space=pltpu.SMEM), vmem, halves, halves],
        out_specs=(
            pl.BlockSpec((tile, WIDE), lambda i: (i, 0)),
            pl.BlockSpec((tile, WIDE), lambda i: (i, 0)),
            pl.BlockSpec((tile, 128), lambda i: (i, 0)),
        ),
        scratch_shapes=[pltpu.VMEM((WIDE, tile), F32), pltpu.VMEM((WIDE, tile), F32)],
        compiler_params=pltpu.CompilerParams(vmem_limit_bytes=16 << 20),
        cost_estimate=pl.CostEstimate(flops=8_000_000_000, bytes_accessed=12 << 20, transcendentals=0),
        name="panel_part",
    )(at, w, own, other)


def update_kernel(
    at_ref, w_ref, high_ref, low_ref, edge_ref, cov_ref, field_ref, g_ref, out_ref, fout_ref, a_ref, b_ref, zh_ref, zl_ref, y_ref, sem
):
    quarters, row_groups, block, wide = a_ref.shape
    tile, columns = cov_ref.shape
    width = field_ref.shape[0]
    size = row_groups * block
    own = 2 * block
    step = pl.program_id(0)

    @pl.when(step == 0)
    def _():
        copies = []
        for q in range(quarters):
            hi = (q + 1) * size
            copies.append(pltpu.make_async_copy(g_ref.at[:, pl.ds(q * block, block), :], a_ref.at[q], sem.at[0, q]))
            copies.append(pltpu.make_async_copy(w_ref.at[pl.ds(q * size, size), :hi], b_ref.at[q, :, :hi], sem.at[1, q]))
        for copy in copies:
            copy.start()
        for q in range(quarters):
            copies[2 * q].wait()
            copies[2 * q + 1].wait()
            lo, hi = q * size, (q + 1) * size
            z = mm(b_ref[q, :, :hi], a_ref[: q + 1].reshape(hi, wide))
            zh_ref[lo:hi, :], zl_ref[lo:hi, :] = split(z)
            y_ref[lo:hi, :] = z[:, columns:]

    def dot(a, b):
        return jnp.dot(a, b, preferred_element_type=F32)

    x_high, x_low = high_ref[...], low_ref[...]
    z_high, z_low = zh_ref[...], zl_ref[...]
    change = dot(x_high, z_high) + (dot(x_high, z_low) + dot(x_low, z_high))
    local = lax.broadcasted_iota(jnp.int32, (tile, 1), 0) + step * tile
    rows = (local // block * row_groups + at_ref[0]) * block + local % block
    out_ref[...] = jnp.where(rows < WIDE, 0.0, cov_ref[...] - change[:, :columns])
    out_ref[:, :own] = edge_ref[:, :own]
    fout_ref[...] = field_ref[...] - change[:, columns:].T[:width]

    @pl.when(step == 0)
    def _():
        mine = [y_ref[pl.ds(pl.multiple_of(q * size + at_ref[0] * block, block), block), :] for q in range(quarters)]
        fout_ref[:, : quarters * block] = jnp.concatenate(mine, axis=0).T[:width]


def update_part(at, w, high, low, edge, covariance, fields, gathered):
    tile = 256
    row_groups, top, wide = gathered.shape
    local_rows, columns = covariance.shape
    width = fields.shape[0]
    quarters = WIDE // 256
    block = top // quarters
    by_rows = lambda i: (i, 0)
    return pl.pallas_call(
        update_kernel,
        grid=(local_rows // tile,),
        out_shape=(
            jax.ShapeDtypeStruct(covariance.shape, F32),
            jax.ShapeDtypeStruct(fields.shape, F32),
        ),
        in_specs=[
            pl.BlockSpec(memory_space=pltpu.SMEM),
            pl.BlockSpec(memory_space=pltpu.HBM),
            pl.BlockSpec((tile, WIDE), by_rows),
            pl.BlockSpec((tile, WIDE), by_rows),
            pl.BlockSpec((tile, 128), by_rows),
            pl.BlockSpec((tile, columns), by_rows),
            pl.BlockSpec((width, tile), lambda i: (0, i)),
            pl.BlockSpec(memory_space=pltpu.HBM),
        ],
        out_specs=(
            pl.BlockSpec((tile, columns), by_rows),
            pl.BlockSpec((width, tile), lambda i: (0, i)),
        ),
        scratch_shapes=[
            pltpu.VMEM((quarters, row_groups, block, wide), F32),
            pltpu.VMEM((quarters, 256, WIDE), F32),
            pltpu.VMEM((WIDE, wide), BF16),
            pltpu.VMEM((WIDE, wide), BF16),
            pltpu.VMEM((WIDE, wide - columns), F32),
            pltpu.SemaphoreType.DMA((2, quarters)),
        ],
        compiler_params=pltpu.CompilerParams(vmem_limit_bytes=62 << 20),
        cost_estimate=pl.CostEstimate(flops=9_000_000_000, bytes_accessed=16 << 20, transcendentals=0),
        name="update_part",
    )(at, w, high, low, edge, covariance, fields, gathered)


def spread_out(piece, axis, count, groups=None):
    copies = jnp.broadcast_to(piece[None], (count,) + piece.shape)
    return lax.all_to_all(copies, axis, 0, 0, axis_index_groups=groups, tiled=True)


def finish(at, covariance, fields, own_pieces, other_pieces, own_panel, other_panel, across):
    w = inverse_factor(at, own_pieces, other_pieces)
    high, low, edge = panel_part(at, w, own_panel, other_panel)
    return update_part(at, w, high, low, edge, covariance, fields, across)


def shards(covariance, fields):
    rows_n = lax.axis_size("row")
    cols_n = lax.axis_size("col")
    at = jnp.stack([lax.axis_index("row"), lax.axis_index("col")]).astype(jnp.int32)
    local_rows, local_columns = covariance.shape
    width = fields.shape[0]
    block = NB // cols_n
    top = WIDE // rows_n
    own = 2 * block
    quarters = top // block
    cores = 2
    same_core = [[cores * i + k for i in range(cols_n // cores)] for k in range(cores)]
    partner = [(i, i ^ 1) for i in range(cols_n)]

    corner = covariance[:top, :own]
    packed = jnp.concatenate([corner[q * block : (q + 1) * block] for q in range(quarters)], axis=1)
    panel = covariance[:, :own].T.reshape(2, block, local_rows)
    own_panel = lax.all_gather(panel, "col", axis=0, axis_index_groups=same_core)

    tall = spread_out(packed, "row", rows_n).reshape(rows_n * block, quarters * own).T
    strip = jnp.concatenate([tall[q * own : (q + 1) * own] for q in range(quarters)], axis=1)
    strip = jnp.concatenate([strip[:block], strip[block:, NB:]], axis=1)

    across = jnp.concatenate([covariance[:top], jnp.pad(fields[:, :top].T, ((0, 0), (0, 128 - width)))], axis=1)
    across, strip = lax.optimization_barrier((across, strip))
    across = lax.all_gather(across, "row", axis=0)

    own_pieces = spread_out(strip, "col", cols_n // cores, same_core)
    own_pieces, own_panel = lax.optimization_barrier((own_pieces, own_panel))
    other_pieces = lax.ppermute(own_pieces, "col", partner)
    other_panel = lax.ppermute(own_panel, "col", partner)
    return finish(at, covariance, fields, own_pieces, other_pieces, own_panel, other_panel, across)


def solution(mesh):
    return jax.shard_map(
        shards,
        mesh=mesh,
        in_specs=(P("row", "col"), P("col", "row")),
        out_specs=(P("row", "col"), P("col", "row")),
        check_vma=False,
    )
```

```python
import functools

import jax
import jax.numpy as jnp
from jax import lax
from jax.experimental import pallas as pl
from jax.experimental.pallas import tpu as pltpu
from jax.sharding import PartitionSpec as P

F32 = jnp.float32
BF16 = jnp.bfloat16
HI = lax.Precision.HIGHEST
NB = 512
WIDE = 2 * NB


def mm(a, b):
    return lax.dot_general(a, b, (((1,), (0,)), ((), ())), precision=HI, preferred_element_type=F32)

def tmm(a, b):
    return lax.dot_general(a, b, (((0,), (0,)), ((), ())), precision=HI, preferred_element_type=F32)

def eliminate(t, out_ref, rows=32, size=128):
    lane = lax.broadcasted_iota(jnp.int32, (8, size), 1)
    sub = lax.broadcasted_iota(jnp.int32, (8, size), 0)
    nv = rows // 8
    for p in range(size // rows):
        k0 = p * rows
        R = [t[8 * v:8 * v + 8, :] for v in range(nv)]
        for s in range(nv):
            c0 = k0 + 8 * s
            inside = (lane >= c0) & (lane < c0 + 8)
            B = [[None] * nv for _ in range(8)]
            for j in range(8):
                for v in range(s, nv):
                    B[j][v] = jnp.broadcast_to(R[v][:, c0 + j:c0 + j + 1], (8, size))
            R[s] = jnp.where(inside, jnp.where(lane - c0 == sub, 1.0, 0.0), R[s])
            for v in range(s + 1, nv):
                R[v] = jnp.where(inside, 0.0, R[v])
            scale = jnp.zeros((8, size), F32)
            for j in range(8):
                d = jnp.broadcast_to(B[j][s][j:j + 1, :], (8, size))
                scale = jnp.where(sub == j, d, scale)
                inv = 1.0 / d
                bl = [None] * 8
                for l in range(j + 1, 8):
                    bl[l] = jnp.broadcast_to(B[l][s][j:j + 1, :], (8, size))
                r = jnp.broadcast_to(R[s][j:j + 1, :], (8, size))
                for v in range(s, nv):
                    m = B[j][v] * inv
                    if v == s:
                        m = jnp.where(sub > j, m, 0.0)
                    for l in range(j + 1, 8):
                        B[l][v] = B[l][v] - m * bl[l]
                    R[v] = R[v] - m * r
            R[s] = R[s] * (1.0 / jnp.sqrt(scale))
        panel = jnp.concatenate(R, axis=0) if nv > 1 else R[0]
        out_ref[k0:k0 + rows, :] = panel
        k1 = k0 + rows
        if k1 < size:
            lane_r = lax.broadcasted_iota(jnp.int32, (rows, size), 1)
            rest = t[rows:, :]
            lr = lax.broadcasted_iota(jnp.int32, rest.shape, 1)
            rest = jnp.where((lr >= k0) & (lr < k1), 0.0, rest)
            sub_r = lax.broadcasted_iota(jnp.int32, (rows, size), 0)
            right = jnp.where((lane_r < k1) & (lane_r - k0 > sub_r), 0.0, panel)
            up = tmm(panel, right)
            t = rest - up[k1:, :]

def diagonal(block_of, w2, blk):
    tri = (lax.broadcasted_iota(jnp.int32, (128, 128), 0) >= lax.broadcasted_iota(jnp.int32, (128, 128), 1))

    eliminate(block_of(0, 0), blk)
    waa = jnp.where(tri, blk[...], 0.0)
    w2[0:128, 0:128] = waa
    w2[0:128, 128:256] = jnp.zeros((128, 128), F32)
    uab = mm(waa, block_of(0, 1))
    vba = -tmm(uab, waa)
    eliminate(block_of(1, 1) - tmm(uab, uab), blk)
    wbb = jnp.where(tri, blk[...], 0.0)
    w2[128:256, 128:256] = wbb
    w2[128:256, 0:128] = mm(wbb, vba)


def factor_step(w_ref, w2, rbuf, blk):
    nb = 256
    steps = WIDE // nb

    def outer(k, _):
        o = pl.multiple_of(k * nb, nb)
        halves = [pl.ds(pl.multiple_of(o + h * 128, 128), 128) for h in range(2)]
        diagonal(lambda i, j: w_ref[halves[i], halves[j]], w2, blk)
        row = pl.ds(o, nb)

        def scale(c, _):
            col = pl.ds(pl.multiple_of(c * nb, nb), nb)

            @pl.when(c != k)
            def _():
                rbuf[:, col] = mm(w2[...], w_ref[row, col])

            @pl.when(c == k)
            def _():
                rbuf[:, col] = w2[...]

            @pl.when(c <= k)
            def _():
                w_ref[row, col] = rbuf[:, col]

            @pl.when(c > k)
            def _():
                w_ref[row, col] = jnp.zeros((nb, nb), F32)
            return 0

        lax.fori_loop(0, steps, scale, 0)

        def below(j, _):
            jo = pl.ds(pl.multiple_of(j * nb, nb), nb)

            def one(c, _):
                col = pl.ds(pl.multiple_of(c * nb, nb), nb)

                @pl.when((c < k) | (c >= j))
                def _():
                    w_ref[jo, col] = w_ref[jo, col] - tmm(rbuf[:, jo], rbuf[:, col])

                @pl.when(c == k)
                def _():
                    w_ref[jo, col] = -tmm(rbuf[:, jo], rbuf[:, col])
                return 0

            lax.fori_loop(0, steps, one, 0)
            return 0

        lax.fori_loop(k + 1, steps, below, 0)
        return 0

    return outer


def first_kernel(at_ref, own_ref, other_ref, w0_ref, w1_ref, w_ref, w2, rbuf, blk):
    chips, block, _ = own_ref.shape
    core = at_ref[1] % 2
    for ref, side in ((own_ref, core), (other_ref, 1 - core)):
        for c in range(chips):
            lo = pl.multiple_of((2 * c + side) * block, block)
            w_ref[pl.ds(lo, block), :] = ref[c, :, 0:WIDE]
            w_ref[pl.ds(NB + lo, block), NB:WIDE] = ref[c, :, WIDE : WIDE + NB]
    w_ref[NB:WIDE, 0:NB] = jnp.zeros((NB, NB), F32)
    lax.fori_loop(0, WIDE // 256 - 1, factor_step(w_ref, w2, rbuf, blk), 0)
    w0_ref[...] = w_ref[:NB, :NB]
    w1_ref[...] = w_ref[NB:, :]


def last_kernel(s_ref, w_ref, w2, blk):
    down, right = NB - 256, WIDE - 256

    def block_of(i, j):
        return w_ref[down + i * 128 : down + i * 128 + 128, right + j * 128 : right + j * 128 + 128]

    diagonal(block_of, w2, blk)
    for c in range(0, right, 256):
        w_ref[down:, c : c + 256] = mm(w2[...], w_ref[down:, c : c + 256])
    w_ref[down:, right:] = w2[...]


def first_steps(at, own, other):
    vmem = pl.BlockSpec(memory_space=pltpu.VMEM)
    return pl.pallas_call(
        first_kernel,
        out_shape=(jax.ShapeDtypeStruct((NB, NB), F32), jax.ShapeDtypeStruct((NB, WIDE), F32)),
        in_specs=[pl.BlockSpec(memory_space=pltpu.SMEM), vmem, vmem],
        out_specs=(vmem, vmem),
        scratch_shapes=[
            pltpu.VMEM((WIDE, WIDE), F32),
            pltpu.VMEM((256, 256), F32),
            pltpu.VMEM((256, WIDE), F32),
            pltpu.VMEM((128, 128), F32),
        ],
        compiler_params=pltpu.CompilerParams(vmem_limit_bytes=12 << 20),
        cost_estimate=pl.CostEstimate(flops=30_000_000_000, bytes_accessed=8 << 20, transcendentals=0),
        name="first_steps",
    )(at, own, other)


def last_step(state):
    vmem = pl.BlockSpec(memory_space=pltpu.VMEM)
    return pl.pallas_call(
        last_kernel,
        out_shape=jax.ShapeDtypeStruct((NB, WIDE), F32),
        in_specs=[vmem],
        out_specs=vmem,
        input_output_aliases={0: 0},
        scratch_shapes=[pltpu.VMEM((256, 256), F32), pltpu.VMEM((128, 128), F32)],
        compiler_params=pltpu.CompilerParams(vmem_limit_bytes=8 << 20),
        cost_estimate=pl.CostEstimate(flops=10_000_000_000, bytes_accessed=4 << 20, transcendentals=0),
        name="last_step",
    )(state)


def split(x):
    high = x.astype(BF16)
    return high, (x - high.astype(F32)).astype(BF16)


def update_kernel(
    at_ref, w0_ref, w1_ref, own_ref, other_ref, g_ref, cov_ref, field_ref, out_ref, fout_ref, p_ref, x_ref, a_ref, zh_ref, zl_ref, y_ref
):
    row_groups, top, wide = g_ref.shape
    chips, _, block, tile = own_ref.shape
    column_groups = 2 * chips
    columns = cov_ref.shape[1]
    width = field_ref.shape[0]
    quarters = top // block
    size = row_groups * block
    own = 2 * block
    step = pl.program_id(0)

    def w(lo):
        hi = lo + size
        return w0_ref[lo:hi, :hi] if hi <= NB else w1_ref[lo - NB : hi - NB, :hi]

    @pl.when(step == 0)
    def _():
        for q in range(quarters):
            lo, hi = q * size, (q + 1) * size
            a_ref[lo:hi, :] = g_ref[:, q * block : (q + 1) * block, :].reshape(size, wide)
            z = mm(w(lo), a_ref[:hi, :])
            zh_ref[lo:hi, :], zl_ref[lo:hi, :] = split(z)
            y_ref[lo:hi, :] = z[:, columns:]

    core = at_ref[1] % 2
    for ref, side in ((own_ref, core), (other_ref, 1 - core)):
        for c in range(chips):
            for p in range(2):
                lo = pl.multiple_of(p * NB + (2 * c + side) * block, block)
                p_ref[pl.ds(lo, block), :] = ref[c, p]
    for i in range(0, WIDE, size):
        x_ref[i : i + size, :] = mm(w(i), p_ref[: i + size, :])

    def dot(a, b):
        return jnp.dot(a, b, preferred_element_type=F32)

    x_high, x_low = split(x_ref[...].T)
    z_high, z_low = zh_ref[...], zl_ref[...]
    change = dot(x_high, z_high) + (dot(x_high, z_low) + dot(x_low, z_high))
    local = lax.broadcasted_iota(jnp.int32, (tile, 1), 0) + step * tile
    rows = (local // block * row_groups + at_ref[0]) * block + local % block
    mine = pl.multiple_of(at_ref[1] * block, block)
    edge = jnp.concatenate([x_ref[pl.ds(mine, block), :], x_ref[pl.ds(NB + mine, block), :]], axis=0).T
    lane = lax.broadcasted_iota(jnp.int32, (1, own), 1)
    lanes = (lane // block * column_groups + at_ref[1]) * block + lane % block
    out_ref[...] = jnp.where(rows < WIDE, 0.0, cov_ref[...] - change[:, :columns])
    out_ref[:, :own] = jnp.where(rows >= lanes, edge, 0.0)
    fout_ref[...] = field_ref[...] - change[:, columns:].T[:width]

    @pl.when(step == 0)
    def _():
        lead = [y_ref[pl.ds(pl.multiple_of(q * size + at_ref[0] * block, block), block), :] for q in range(quarters)]
        fout_ref[:, :top] = jnp.concatenate(lead, axis=0).T[:width]


def update_part(at, w0, w1, own, other, gathered, covariance, fields):
    vmem = pl.BlockSpec(memory_space=pltpu.VMEM)
    tile = 256
    chips, _, block, local_rows = own.shape
    columns = covariance.shape[1]
    width = fields.shape[0]
    wide = gathered.shape[2]
    halves = pl.BlockSpec((chips, 2, block, tile), lambda i: (0, 0, 0, i))
    tiles = [pl.BlockSpec((tile, columns), lambda i: (i, 0)), pl.BlockSpec((width, tile), lambda i: (0, i))]
    return pl.pallas_call(
        update_kernel,
        grid=(local_rows // tile,),
        out_shape=(
            jax.ShapeDtypeStruct(covariance.shape, F32),
            jax.ShapeDtypeStruct(fields.shape, F32),
        ),
        in_specs=[pl.BlockSpec(memory_space=pltpu.SMEM), vmem, vmem, halves, halves, vmem] + tiles,
        out_specs=tuple(tiles),
        scratch_shapes=[
            pltpu.VMEM((WIDE, tile), F32),
            pltpu.VMEM((WIDE, tile), F32),
            pltpu.VMEM((WIDE, wide), F32),
            pltpu.VMEM((WIDE, wide), BF16),
            pltpu.VMEM((WIDE, wide), BF16),
            pltpu.VMEM((WIDE, wide - columns), F32),
        ],
        compiler_params=pltpu.CompilerParams(vmem_limit_bytes=28 << 20),
        cost_estimate=pl.CostEstimate(flops=20_000_000_000, bytes_accessed=16 << 20, transcendentals=0),
        name="update_part",
    )(at, w0, w1, own, other, gathered, covariance, fields)


def spread_out(piece, axis, count, groups=None):
    copies = jnp.broadcast_to(piece[None], (count,) + piece.shape)
    return lax.all_to_all(copies, axis, 0, 0, axis_index_groups=groups, tiled=True)


def finish(at, covariance, fields, own_pieces, other_pieces, own_panel, other_panel, across):
    w0, state = first_steps(at, own_pieces, other_pieces)
    return update_part(at, w0, last_step(state), own_panel, other_panel, across, covariance, fields)


def shards(covariance, fields):
    rows_n = lax.axis_size("row")
    cols_n = lax.axis_size("col")
    at = jnp.stack([lax.axis_index("row"), lax.axis_index("col")]).astype(jnp.int32)
    local_rows, local_columns = covariance.shape
    width = fields.shape[0]
    block = NB // cols_n
    top = WIDE // rows_n
    own = 2 * block
    quarters = top // block
    cores = 2
    chips = cols_n // cores
    same_core = [[cores * i + k for i in range(chips)] for k in range(cores)]

    def swap(x):
        return lax.ppermute(x, "col", [(i, i ^ 1) for i in range(cols_n)])

    corner = covariance[:top, :own]
    packed = jnp.concatenate([corner[q * block : (q + 1) * block] for q in range(quarters)], axis=1)
    across = jnp.concatenate([covariance[:top], jnp.pad(fields[:, :top].T, ((0, 0), (0, 128 - width)))], axis=1)
    packed, across = lax.optimization_barrier((packed, across))
    across = lax.all_gather(across, "row", axis=0)

    tall = spread_out(packed, "row", rows_n).reshape(rows_n * block, quarters * own).T
    strip = jnp.concatenate([tall[q * own : (q + 1) * own] for q in range(quarters)], axis=1)
    strip = jnp.concatenate([strip[:block], strip[block:, NB:]], axis=1)
    own_pieces = spread_out(strip, "col", chips, same_core)
    panel = covariance[:, :own].T.reshape(2, block, local_rows)
    own_pieces, panel = lax.optimization_barrier((own_pieces, panel))
    other_pieces = swap(own_pieces)
    own_panel = spread_out(panel, "col", chips, same_core)
    w0, state = first_steps(at, own_pieces, other_pieces)
    state, own_panel, across = lax.optimization_barrier((state, own_panel, across))
    other_panel = swap(own_panel)
    w1 = last_step(state)
    return update_part(at, w0, w1, own_panel, other_panel, across, covariance, fields)


def solution(mesh):
    return jax.shard_map(
        shards,
        mesh=mesh,
        in_specs=(P("row", "col"), P("col", "row")),
        out_specs=(P("row", "col"), P("col", "row")),
        check_vma=False,
    )
```

```python
import functools

import jax
import jax.numpy as jnp
from jax import lax
from jax.experimental import pallas as pl
from jax.experimental.pallas import tpu as pltpu
from jax.sharding import PartitionSpec as P

F32 = jnp.float32
BF16 = jnp.bfloat16
HI = lax.Precision.HIGHEST
NB = 512
WIDE = 2 * NB


def mm(a, b):
    return lax.dot_general(a, b, (((1,), (0,)), ((), ())), precision=HI, preferred_element_type=F32)

def tmm(a, b):
    return lax.dot_general(a, b, (((0,), (0,)), ((), ())), precision=HI, preferred_element_type=F32)

def eliminate(t, out_ref, rows=64, size=128):
    lane = lax.broadcasted_iota(jnp.int32, (8, size), 1)
    sub = lax.broadcasted_iota(jnp.int32, (8, size), 0)
    nv = rows // 8
    for p in range(size // rows):
        k0 = p * rows
        R = [t[8 * v:8 * v + 8, :] for v in range(nv)]
        for s in range(nv):
            c0 = k0 + 8 * s
            inside = (lane >= c0) & (lane < c0 + 8)
            B = [[None] * nv for _ in range(8)]
            for j in range(8):
                for v in range(s, nv):
                    B[j][v] = jnp.broadcast_to(R[v][:, c0 + j:c0 + j + 1], (8, size))
                B[j][s] = jnp.where(lane < size + j, B[j][s], 0.0)
            U = [[jnp.broadcast_to(B[l][s][i:i + 1, :], (8, size)) if i >= l else None for i in range(8)] for l in range(8)]
            R[s] = jnp.where(inside, jnp.where(lane - c0 == sub, 1.0, 0.0), R[s])
            for v in range(s + 1, nv):
                R[v] = jnp.where(inside, 0.0, R[v])
            scale = jnp.zeros((8, size), F32)
            for j in range(8):
                d = U[j][j]
                scale = jnp.where(sub == j, d, scale)
                inv = 1.0 / d
                for i in range(j + 1, 8):
                    f = U[j][i] * inv
                    for l in range(j + 1, i + 1):
                        U[l][i] = U[l][i] - f * U[j][l]
                r = jnp.broadcast_to(R[s][j:j + 1, :], (8, size))
                for v in range(s, nv):
                    m = B[j][v] * inv
                    if v == s:
                        m = jnp.where(sub > j, m, 0.0)
                    for l in range(j + 1, 8):
                        B[l][v] = B[l][v] - m * U[j][l]
                    R[v] = R[v] - m * r
            R[s] = R[s] * (1.0 / jnp.sqrt(scale))
        panel = jnp.concatenate(R, axis=0) if nv > 1 else R[0]
        out_ref[k0:k0 + rows, :] = panel
        k1 = k0 + rows
        if k1 < size:
            lane_r = lax.broadcasted_iota(jnp.int32, (rows, size), 1)
            rest = t[rows:, :]
            lr = lax.broadcasted_iota(jnp.int32, rest.shape, 1)
            rest = jnp.where((lr >= k0) & (lr < k1), 0.0, rest)
            sub_r = lax.broadcasted_iota(jnp.int32, (rows, size), 0)
            right = jnp.where((lane_r < k1) & (lane_r - k0 > sub_r), 0.0, panel)
            t = rest - mm(panel.T[k1:, :], right)


def diagonal(block_of, w2, blk):
    tri = (lax.broadcasted_iota(jnp.int32, (128, 128), 0) >= lax.broadcasted_iota(jnp.int32, (128, 128), 1))

    eliminate(block_of(0, 0), blk)
    waa = jnp.where(tri, blk[...], 0.0)
    w2[0:128, 0:128] = waa
    w2[0:128, 128:256] = jnp.zeros((128, 128), F32)
    uab = mm(waa, block_of(0, 1))
    vba = -tmm(uab, waa)
    eliminate(block_of(1, 1) - tmm(uab, uab), blk)
    wbb = jnp.where(tri, blk[...], 0.0)
    w2[128:256, 128:256] = wbb
    w2[128:256, 0:128] = mm(wbb, vba)


def factor_step(w_ref, w2, rbuf, blk):
    nb = 256
    steps = WIDE // nb

    def outer(k, _):
        o = pl.multiple_of(k * nb, nb)
        halves = [pl.ds(pl.multiple_of(o + h * 128, 128), 128) for h in range(2)]
        diagonal(lambda i, j: w_ref[halves[i], halves[j]], w2, blk)
        row = pl.ds(o, nb)

        def scale(c, _):
            col = pl.ds(pl.multiple_of(c * nb, nb), nb)

            @pl.when(c != k)
            def _():
                rbuf[:, col] = mm(w2[...], w_ref[row, col])

            @pl.when(c == k)
            def _():
                rbuf[:, col] = w2[...]

            @pl.when(c <= k)
            def _():
                w_ref[row, col] = rbuf[:, col]

            @pl.when(c > k)
            def _():
                w_ref[row, col] = jnp.zeros((nb, nb), F32)
            return 0

        lax.fori_loop(0, steps, scale, 0)

        def below(j, _):
            jo = pl.ds(pl.multiple_of(j * nb, nb), nb)

            def one(c, _):
                col = pl.ds(pl.multiple_of(c * nb, nb), nb)

                @pl.when((c < k) | (c >= j))
                def _():
                    w_ref[jo, col] = w_ref[jo, col] - tmm(rbuf[:, jo], rbuf[:, col])

                @pl.when(c == k)
                def _():
                    w_ref[jo, col] = -tmm(rbuf[:, jo], rbuf[:, col])
                return 0

            lax.fori_loop(0, steps, one, 0)
            return 0

        lax.fori_loop(k + 1, steps, below, 0)
        return 0

    return outer


def first_kernel(at_ref, own_ref, other_ref, w0_ref, w1_ref, w_ref, w2, rbuf, blk):
    chips, block, _ = own_ref.shape
    core = at_ref[1] % 2
    for ref, side in ((own_ref, core), (other_ref, 1 - core)):
        for c in range(chips):
            lo = pl.multiple_of((2 * c + side) * block, block)
            w_ref[pl.ds(lo, block), :] = ref[c, :, 0:WIDE]
            w_ref[pl.ds(NB + lo, block), NB:WIDE] = ref[c, :, WIDE : WIDE + NB]
    w_ref[NB:WIDE, 0:NB] = jnp.zeros((NB, NB), F32)
    lax.fori_loop(0, WIDE // 256 - 1, factor_step(w_ref, w2, rbuf, blk), 0)
    w0_ref[...] = w_ref[:NB, :NB]
    w1_ref[...] = w_ref[NB:, :]


def last_kernel(s_ref, w_ref, w2, blk):
    down, right = NB - 256, WIDE - 256

    def block_of(i, j):
        return w_ref[down + i * 128 : down + i * 128 + 128, right + j * 128 : right + j * 128 + 128]

    diagonal(block_of, w2, blk)
    for c in range(0, right, 256):
        w_ref[down:, c : c + 256] = mm(w2[...], w_ref[down:, c : c + 256])
    w_ref[down:, right:] = w2[...]


def first_steps(at, own, other):
    vmem = pl.BlockSpec(memory_space=pltpu.VMEM)
    return pl.pallas_call(
        first_kernel,
        out_shape=(jax.ShapeDtypeStruct((NB, NB), F32), jax.ShapeDtypeStruct((NB, WIDE), F32)),
        in_specs=[pl.BlockSpec(memory_space=pltpu.SMEM), vmem, vmem],
        out_specs=(vmem, vmem),
        scratch_shapes=[
            pltpu.VMEM((WIDE, WIDE), F32),
            pltpu.VMEM((256, 256), F32),
            pltpu.VMEM((256, WIDE), F32),
            pltpu.VMEM((128, 128), F32),
        ],
        compiler_params=pltpu.CompilerParams(vmem_limit_bytes=12 << 20),
        cost_estimate=pl.CostEstimate(flops=30_000_000_000, bytes_accessed=8 << 20, transcendentals=0),
        name="first_steps",
    )(at, own, other)


def last_step(state):
    vmem = pl.BlockSpec(memory_space=pltpu.VMEM)
    return pl.pallas_call(
        last_kernel,
        out_shape=jax.ShapeDtypeStruct((NB, WIDE), F32),
        in_specs=[vmem],
        out_specs=vmem,
        input_output_aliases={0: 0},
        scratch_shapes=[pltpu.VMEM((256, 256), F32), pltpu.VMEM((128, 128), F32)],
        compiler_params=pltpu.CompilerParams(vmem_limit_bytes=8 << 20),
        cost_estimate=pl.CostEstimate(flops=10_000_000_000, bytes_accessed=4 << 20, transcendentals=0),
        name="last_step",
    )(state)


def split3(x):
    high = x.astype(BF16)
    rest = x - high.astype(F32)
    middle = rest.astype(BF16)
    return high, middle, (rest - middle.astype(F32)).astype(BF16)


def dot(a, b):
    return jnp.dot(a, b, preferred_element_type=F32)


def six(a, b, by):
    (ah, am, al), (bh, bm, bl) = a, b
    return ((by(am, bm) + by(ah, bl) + by(al, bh)) + (by(ah, bm) + by(am, bh))) + by(ah, bh)


def across_dot(a, b):
    return lax.dot_general(a, b, (((1,), (1,)), ((), ())), preferred_element_type=F32)


def update_kernel(
    at_ref, w0_ref, w1_ref, own_ref, other_ref, g_ref, cov_ref, field_ref, out_ref, fout_ref, x_ref, w_ref, a_ref, p_ref, z_ref, y_ref
):
    row_groups, top, wide = g_ref.shape
    chips, _, block, tile = own_ref.shape
    column_groups = 2 * chips
    columns = cov_ref.shape[1]
    width = field_ref.shape[0]
    used = columns + width
    quarters = top // block
    size = row_groups * block
    own = 2 * block
    step = pl.program_id(0)

    def take(ref, *index):
        return [ref[(n,) + index] for n in range(3)]

    def put(ref, value, *index):
        for n, term in enumerate(split3(value)):
            ref[(n,) + index] = term

    @pl.when(step == 0)
    def _():
        for q in range(quarters):
            lo, hi = q * size, (q + 1) * size
            rows, cols = slice(lo, hi), slice(0, hi)
            put(w_ref, w0_ref[rows, cols] if hi <= NB else w1_ref[lo - NB : hi - NB, cols], rows, cols)
            lead = g_ref[:, q * block : (q + 1) * block, :].reshape(size, wide)
            put(a_ref, lead.T[:used], slice(0, used), rows)
            z = six(take(a_ref, slice(0, used), cols), take(w_ref, rows, cols), across_dot)
            put(z_ref, z, slice(0, used), rows)
            y_ref[rows, :width] = z[columns:].T

    even = at_ref[1] % 2 == 0
    for p in range(2):
        for c in range(chips):
            mine, yours = own_ref[c, p], other_ref[c, p]
            lo = p * NB + 2 * c * block
            put(p_ref, jnp.where(even, mine, yours), slice(lo, lo + block))
            put(p_ref, jnp.where(even, yours, mine), slice(lo + block, lo + own))
    for i in range(0, WIDE, size):
        rows, cols = slice(i, i + size), slice(0, i + size)
        x_ref[rows, :] = six(take(w_ref, rows, cols), take(p_ref, cols), dot)

    change = six([z_ref[n] for n in range(3)], split3(x_ref[...]), dot)
    local = lax.broadcasted_iota(jnp.int32, (tile, 1), 0) + step * tile
    rows = (local // block * row_groups + at_ref[0]) * block + local % block
    mine = pl.multiple_of(at_ref[1] * block, block)
    edge = jnp.concatenate([x_ref[pl.ds(mine, block), :], x_ref[pl.ds(NB + mine, block), :]], axis=0).T
    lane = lax.broadcasted_iota(jnp.int32, (1, own), 1)
    lanes = (lane // block * column_groups + at_ref[1]) * block + lane % block
    out_ref[...] = jnp.where(rows < WIDE, 0.0, cov_ref[...] - change[:columns].T)
    out_ref[:, :own] = jnp.where(rows >= lanes, edge, 0.0)
    fout_ref[...] = field_ref[...] - change[columns:]

    @pl.when(step == 0)
    def _():
        lead = [y_ref[pl.ds(pl.multiple_of(q * size + at_ref[0] * block, block), block), :] for q in range(quarters)]
        fout_ref[:, :top] = jnp.concatenate(lead, axis=0).T[:width]


def update_part(at, w0, w1, own, other, gathered, covariance, fields):
    vmem = pl.BlockSpec(memory_space=pltpu.VMEM)
    tile = 256
    chips, _, block, local_rows = own.shape
    columns = covariance.shape[1]
    width = fields.shape[0]
    wide = gathered.shape[2]
    halves = pl.BlockSpec((chips, 2, block, tile), lambda i: (0, 0, 0, i))
    tiles = [pl.BlockSpec((tile, columns), lambda i: (i, 0)), pl.BlockSpec((width, tile), lambda i: (0, i))]
    return pl.pallas_call(
        update_kernel,
        grid=(local_rows // tile,),
        out_shape=(
            jax.ShapeDtypeStruct(covariance.shape, F32),
            jax.ShapeDtypeStruct(fields.shape, F32),
        ),
        in_specs=[pl.BlockSpec(memory_space=pltpu.SMEM), vmem, vmem, halves, halves, vmem] + tiles,
        out_specs=tuple(tiles),
        scratch_shapes=[
            pltpu.VMEM((WIDE, tile), F32),
            pltpu.VMEM((3, WIDE, WIDE), BF16),
            pltpu.VMEM((3, columns + width, WIDE), BF16),
            pltpu.VMEM((3, WIDE, tile), BF16),
            pltpu.VMEM((3, columns + width, WIDE), BF16),
            pltpu.VMEM((WIDE, 128), F32),
        ],
        compiler_params=pltpu.CompilerParams(vmem_limit_bytes=28 << 20),
        cost_estimate=pl.CostEstimate(flops=20_000_000_000, bytes_accessed=16 << 20, transcendentals=0),
        name="update_part",
    )(at, w0, w1, own, other, gathered, covariance, fields)


def spread_out(piece, axis, count, groups=None):
    copies = jnp.broadcast_to(piece[None], (count,) + piece.shape)
    return lax.all_to_all(copies, axis, 0, 0, axis_index_groups=groups, tiled=True)


def finish(at, covariance, fields, own_pieces, other_pieces, own_panel, other_panel, across):
    w0, state = first_steps(at, own_pieces, other_pieces)
    return update_part(at, w0, last_step(state), own_panel, other_panel, across, covariance, fields)


def shards(covariance, fields):
    rows_n = lax.axis_size("row")
    cols_n = lax.axis_size("col")
    at = jnp.stack([lax.axis_index("row"), lax.axis_index("col")]).astype(jnp.int32)
    local_rows, local_columns = covariance.shape
    width = fields.shape[0]
    block = NB // cols_n
    top = WIDE // rows_n
    own = 2 * block
    quarters = top // block
    cores = 2
    chips = cols_n // cores
    same_core = [[cores * i + k for i in range(chips)] for k in range(cores)]

    def swap(x):
        return lax.ppermute(x, "col", [(i, i ^ 1) for i in range(cols_n)])

    corner = covariance[:top, :own]
    packed = jnp.concatenate([corner[q * block : (q + 1) * block] for q in range(quarters)], axis=1)
    across = jnp.concatenate([covariance[:top], jnp.pad(fields[:, :top].T, ((0, 0), (0, 128 - width)))], axis=1)
    packed, across = lax.optimization_barrier((packed, across))
    across = lax.all_gather(across, "row", axis=0)

    tall = spread_out(packed, "row", rows_n).reshape(rows_n * block, quarters * own).T
    strip = jnp.concatenate([tall[q * own : (q + 1) * own] for q in range(quarters)], axis=1)
    strip = jnp.concatenate([strip[:block], strip[block:, NB:]], axis=1)
    own_pieces = spread_out(strip, "col", chips, same_core)
    panel = covariance[:, :own].T.reshape(2, block, local_rows)
    own_pieces, panel = lax.optimization_barrier((own_pieces, panel))
    other_pieces = swap(own_pieces)
    own_panel = spread_out(panel, "col", chips, same_core)
    w0, state = first_steps(at, own_pieces, other_pieces)
    state, own_panel, across = lax.optimization_barrier((state, own_panel, across))
    other_panel = swap(own_panel)
    w1 = last_step(state)
    return update_part(at, w0, w1, own_panel, other_panel, across, covariance, fields)


def solution(mesh):
    return jax.shard_map(
        shards,
        mesh=mesh,
        in_specs=(P("row", "col"), P("col", "row")),
        out_specs=(P("row", "col"), P("col", "row")),
        check_vma=False,
    )
```

```python
import functools

import jax
import jax.numpy as jnp
from jax import lax
from jax.experimental import pallas as pl
from jax.experimental.pallas import tpu as pltpu
from jax.sharding import PartitionSpec as P

F32 = jnp.float32
BF16 = jnp.bfloat16
HI = lax.Precision.HIGHEST
NB = 512
WIDE = 2 * NB


def mm(a, b):
    return lax.dot_general(a, b, (((1,), (0,)), ((), ())), precision=HI, preferred_element_type=F32)

def tmm(a, b):
    return lax.dot_general(a, b, (((0,), (0,)), ((), ())), precision=HI, preferred_element_type=F32)

def eliminate(t, out_ref, rows=64, size=128):
    lane = lax.broadcasted_iota(jnp.int32, (8, size), 1)
    sub = lax.broadcasted_iota(jnp.int32, (8, size), 0)
    nv = rows // 8
    for p in range(size // rows):
        k0 = p * rows
        R = [t[8 * v:8 * v + 8, :] for v in range(nv)]
        for s in range(nv):
            c0 = k0 + 8 * s
            inside = (lane >= c0) & (lane < c0 + 8)
            B = [[None] * nv for _ in range(8)]
            for j in range(8):
                for v in range(s, nv):
                    B[j][v] = jnp.broadcast_to(R[v][:, c0 + j:c0 + j + 1], (8, size))
                B[j][s] = jnp.where(lane < size + j, B[j][s], 0.0)
            U = [[jnp.broadcast_to(B[l][s][i:i + 1, :], (8, size)) if i >= l else None for i in range(8)] for l in range(8)]
            R[s] = jnp.where(inside, jnp.where(lane - c0 == sub, 1.0, 0.0), R[s])
            for v in range(s + 1, nv):
                R[v] = jnp.where(inside, 0.0, R[v])
            scale = jnp.zeros((8, size), F32)
            for j in range(8):
                d = U[j][j]
                scale = jnp.where(sub == j, d, scale)
                inv = 1.0 / d
                for i in range(j + 1, 8):
                    f = U[j][i] * inv
                    for l in range(j + 1, i + 1):
                        U[l][i] = U[l][i] - f * U[j][l]
                r = jnp.broadcast_to(R[s][j:j + 1, :], (8, size))
                for v in range(s, nv):
                    m = B[j][v] * inv
                    if v == s:
                        m = jnp.where(sub > j, m, 0.0)
                    for l in range(j + 1, 8):
                        B[l][v] = B[l][v] - m * U[j][l]
                    R[v] = R[v] - m * r
            R[s] = R[s] * (1.0 / jnp.sqrt(scale))
        panel = jnp.concatenate(R, axis=0) if nv > 1 else R[0]
        out_ref[k0:k0 + rows, :] = panel
        k1 = k0 + rows
        if k1 < size:
            lane_r = lax.broadcasted_iota(jnp.int32, (rows, size), 1)
            rest = t[rows:, :]
            lr = lax.broadcasted_iota(jnp.int32, rest.shape, 1)
            rest = jnp.where((lr >= k0) & (lr < k1), 0.0, rest)
            sub_r = lax.broadcasted_iota(jnp.int32, (rows, size), 0)
            right = jnp.where((lane_r < k1) & (lane_r - k0 > sub_r), 0.0, panel)
            t = rest - mm(panel.T[k1:, :], right)


def diagonal(block_of, w2, blk):
    tri = (lax.broadcasted_iota(jnp.int32, (128, 128), 0) >= lax.broadcasted_iota(jnp.int32, (128, 128), 1))

    eliminate(block_of(0, 0), blk)
    waa = jnp.where(tri, blk[...], 0.0)
    w2[0:128, 0:128] = waa
    w2[0:128, 128:256] = jnp.zeros((128, 128), F32)
    uab = mm(waa, block_of(0, 1))
    vba = -tmm(uab, waa)
    eliminate(block_of(1, 1) - tmm(uab, uab), blk)
    wbb = jnp.where(tri, blk[...], 0.0)
    w2[128:256, 128:256] = wbb
    w2[128:256, 0:128] = mm(wbb, vba)


def factor_step(w_ref, w2, rbuf, blk):
    nb = 256
    steps = WIDE // nb

    def outer(k, _):
        o = pl.multiple_of(k * nb, nb)
        halves = [pl.ds(pl.multiple_of(o + h * 128, 128), 128) for h in range(2)]
        diagonal(lambda i, j: w_ref[halves[i], halves[j]], w2, blk)
        row = pl.ds(o, nb)

        def scale(c, _):
            col = pl.ds(pl.multiple_of(c * nb, nb), nb)

            @pl.when(c != k)
            def _():
                rbuf[:, col] = mm(w2[...], w_ref[row, col])

            @pl.when(c == k)
            def _():
                rbuf[:, col] = w2[...]

            @pl.when(c <= k)
            def _():
                w_ref[row, col] = rbuf[:, col]

            @pl.when(c > k)
            def _():
                w_ref[row, col] = jnp.zeros((nb, nb), F32)
            return 0

        lax.fori_loop(0, steps, scale, 0)

        def below(j, _):
            jo = pl.ds(pl.multiple_of(j * nb, nb), nb)

            def one(c, _):
                col = pl.ds(pl.multiple_of(c * nb, nb), nb)

                @pl.when((c < k) | (c >= j))
                def _():
                    w_ref[jo, col] = w_ref[jo, col] - tmm(rbuf[:, jo], rbuf[:, col])

                @pl.when(c == k)
                def _():
                    w_ref[jo, col] = -tmm(rbuf[:, jo], rbuf[:, col])
                return 0

            lax.fori_loop(0, steps, one, 0)
            return 0

        lax.fori_loop(k + 1, steps, below, 0)
        return 0

    return outer


def first_kernel(at_ref, own_ref, other_ref, w0_ref, w1_ref, state_ref, w_ref, w2, rbuf, blk):
    chips, block, _ = own_ref.shape
    core = at_ref[1] % 2
    for ref, side in ((own_ref, core), (other_ref, 1 - core)):
        for c in range(chips):
            lo = pl.multiple_of((2 * c + side) * block, block)
            w_ref[pl.ds(lo, block), :] = ref[c, :, 0:WIDE]
            w_ref[pl.ds(NB + lo, block), NB:WIDE] = ref[c, :, WIDE : WIDE + NB]
    w_ref[NB:WIDE, 0:NB] = jnp.zeros((NB, NB), F32)
    lax.fori_loop(0, WIDE // 256 - 1, factor_step(w_ref, w2, rbuf, blk), 0)
    w0_ref[...] = w_ref[:NB, :NB]
    w1_ref[...] = w_ref[NB : WIDE - 256, :]
    state_ref[...] = w_ref[WIDE - 256 :, :]


def last_kernel(s_ref, w_ref, w2, blk):
    right = WIDE - 256

    def block_of(i, j):
        return w_ref[i * 128 : i * 128 + 128, right + j * 128 : right + j * 128 + 128]

    diagonal(block_of, w2, blk)
    for c in range(0, right, 256):
        w_ref[:, c : c + 256] = mm(w2[...], w_ref[:, c : c + 256])
    w_ref[:, right:] = w2[...]


def first_steps(at, own, other):
    vmem = pl.BlockSpec(memory_space=pltpu.VMEM)
    return pl.pallas_call(
        first_kernel,
        out_shape=(
            jax.ShapeDtypeStruct((NB, NB), F32),
            jax.ShapeDtypeStruct((256, WIDE), F32),
            jax.ShapeDtypeStruct((256, WIDE), F32),
        ),
        in_specs=[pl.BlockSpec(memory_space=pltpu.SMEM), vmem, vmem],
        out_specs=(vmem, vmem, vmem),
        scratch_shapes=[
            pltpu.VMEM((WIDE, WIDE), F32),
            pltpu.VMEM((256, 256), F32),
            pltpu.VMEM((256, WIDE), F32),
            pltpu.VMEM((128, 128), F32),
        ],
        compiler_params=pltpu.CompilerParams(vmem_limit_bytes=12 << 20),
        cost_estimate=pl.CostEstimate(flops=30_000_000_000, bytes_accessed=8 << 20, transcendentals=0),
        name="first_steps",
    )(at, own, other)


def last_step(state):
    vmem = pl.BlockSpec(memory_space=pltpu.VMEM)
    return pl.pallas_call(
        last_kernel,
        out_shape=jax.ShapeDtypeStruct((256, WIDE), F32),
        in_specs=[vmem],
        out_specs=vmem,
        input_output_aliases={0: 0},
        scratch_shapes=[pltpu.VMEM((256, 256), F32), pltpu.VMEM((128, 128), F32)],
        compiler_params=pltpu.CompilerParams(vmem_limit_bytes=8 << 20),
        cost_estimate=pl.CostEstimate(flops=10_000_000_000, bytes_accessed=4 << 20, transcendentals=0),
        name="last_step",
    )(state)


def split3(x):
    high = x.astype(BF16)
    rest = x - high.astype(F32)
    middle = rest.astype(BF16)
    return high, middle, (rest - middle.astype(F32)).astype(BF16)


def dot(a, b):
    return jnp.dot(a, b, preferred_element_type=F32)


def six(a, b, by):
    (ah, am, al), (bh, bm, bl) = a, b
    return ((by(am, bm) + by(ah, bl) + by(al, bh)) + (by(ah, bm) + by(am, bh))) + by(ah, bh)


def across_dot(a, b):
    return lax.dot_general(a, b, (((1,), (1,)), ((), ())), preferred_element_type=F32)


def update_kernel(
    at_ref, w0_ref, w1_ref, w2_ref, own_ref, other_ref, g_ref, cov_ref, field_ref, out_ref, fout_ref, x_ref, w_ref, a_ref, p_ref, z_ref, y_ref
):
    row_groups, top, wide = g_ref.shape
    chips, _, block, tile = own_ref.shape
    column_groups = 2 * chips
    columns = cov_ref.shape[1]
    width = field_ref.shape[0]
    used = columns + width
    quarters = top // block
    size = row_groups * block
    own = 2 * block
    step = pl.program_id(0)

    def take(ref, *index):
        return [ref[(n,) + index] for n in range(3)]

    def put(ref, value, *index):
        for n, term in enumerate(split3(value)):
            ref[(n,) + index] = term

    @pl.when(step == 0)
    def _():
        for q in range(quarters):
            lo, hi = q * size, (q + 1) * size
            rows, cols = slice(lo, hi), slice(0, hi)
            put(w_ref, w0_ref[rows, cols] if hi <= NB else (w1_ref, w2_ref)[q - 2][:, cols], rows, cols)
            lead = g_ref[:, q * block : (q + 1) * block, :].reshape(size, wide)
            put(a_ref, lead.T[:used], slice(0, used), rows)
            z = six(take(a_ref, slice(0, used), cols), take(w_ref, rows, cols), across_dot)
            put(z_ref, z, slice(0, used), rows)
            y_ref[rows, :width] = z[columns:].T

    even = at_ref[1] % 2 == 0
    for p in range(2):
        for c in range(chips):
            mine, yours = own_ref[c, p], other_ref[c, p]
            lo = p * NB + 2 * c * block
            put(p_ref, jnp.where(even, mine, yours), slice(lo, lo + block))
            put(p_ref, jnp.where(even, yours, mine), slice(lo + block, lo + own))
    for i in range(0, WIDE, size):
        rows, cols = slice(i, i + size), slice(0, i + size)
        x_ref[rows, :] = six(take(w_ref, rows, cols), take(p_ref, cols), dot)

    change = six([z_ref[n] for n in range(3)], split3(x_ref[...]), dot)
    local = lax.broadcasted_iota(jnp.int32, (tile, 1), 0) + step * tile
    rows = (local // block * row_groups + at_ref[0]) * block + local % block
    mine = pl.multiple_of(at_ref[1] * block, block)
    edge = jnp.concatenate([x_ref[pl.ds(mine, block), :], x_ref[pl.ds(NB + mine, block), :]], axis=0).T
    lane = lax.broadcasted_iota(jnp.int32, (1, own), 1)
    lanes = (lane // block * column_groups + at_ref[1]) * block + lane % block
    out_ref[...] = jnp.where(rows < WIDE, 0.0, cov_ref[...] - change[:columns].T)
    out_ref[:, :own] = jnp.where(rows >= lanes, edge, 0.0)
    fout_ref[...] = field_ref[...] - change[columns:]

    @pl.when(step == 0)
    def _():
        lead = [y_ref[pl.ds(pl.multiple_of(q * size + at_ref[0] * block, block), block), :] for q in range(quarters)]
        fout_ref[:, :top] = jnp.concatenate(lead, axis=0).T[:width]


def update_part(at, w0, w1, w2, own, other, gathered, covariance, fields):
    vmem = pl.BlockSpec(memory_space=pltpu.VMEM)
    tile = 256
    chips, _, block, local_rows = own.shape
    columns = covariance.shape[1]
    width = fields.shape[0]
    wide = gathered.shape[2]
    halves = pl.BlockSpec((chips, 2, block, tile), lambda i: (0, 0, 0, i))
    tiles = [pl.BlockSpec((tile, columns), lambda i: (i, 0)), pl.BlockSpec((width, tile), lambda i: (0, i))]
    return pl.pallas_call(
        update_kernel,
        grid=(local_rows // tile,),
        out_shape=(
            jax.ShapeDtypeStruct(covariance.shape, F32),
            jax.ShapeDtypeStruct(fields.shape, F32),
        ),
        in_specs=[pl.BlockSpec(memory_space=pltpu.SMEM), vmem, vmem, vmem, halves, halves, vmem] + tiles,
        out_specs=tuple(tiles),
        scratch_shapes=[
            pltpu.VMEM((WIDE, tile), F32),
            pltpu.VMEM((3, WIDE, WIDE), BF16),
            pltpu.VMEM((3, columns + width, WIDE), BF16),
            pltpu.VMEM((3, WIDE, tile), BF16),
            pltpu.VMEM((3, columns + width, WIDE), BF16),
            pltpu.VMEM((WIDE, 128), F32),
        ],
        compiler_params=pltpu.CompilerParams(vmem_limit_bytes=28 << 20),
        cost_estimate=pl.CostEstimate(flops=20_000_000_000, bytes_accessed=16 << 20, transcendentals=0),
        name="update_part",
    )(at, w0, w1, w2, own, other, gathered, covariance, fields)


def spread_out(piece, axis, count, groups=None):
    copies = jnp.broadcast_to(piece[None], (count,) + piece.shape)
    return lax.all_to_all(copies, axis, 0, 0, axis_index_groups=groups, tiled=True)


def finish(at, covariance, fields, own_pieces, other_pieces, own_panel, other_panel, across):
    w0, w1, state = first_steps(at, own_pieces, other_pieces)
    return update_part(at, w0, w1, last_step(state), own_panel, other_panel, across, covariance, fields)


def shards(covariance, fields):
    rows_n = lax.axis_size("row")
    cols_n = lax.axis_size("col")
    at = jnp.stack([lax.axis_index("row"), lax.axis_index("col")]).astype(jnp.int32)
    local_rows, local_columns = covariance.shape
    width = fields.shape[0]
    block = NB // cols_n
    top = WIDE // rows_n
    own = 2 * block
    quarters = top // block
    cores = 2
    chips = cols_n // cores
    same_core = [[cores * i + k for i in range(chips)] for k in range(cores)]

    def swap(x):
        return lax.ppermute(x, "col", [(i, i ^ 1) for i in range(cols_n)])

    corner = covariance[:top, :own]
    packed = jnp.concatenate([corner[q * block : (q + 1) * block] for q in range(quarters)], axis=1)
    across = jnp.concatenate([covariance[:top], jnp.pad(fields[:, :top].T, ((0, 0), (0, 128 - width)))], axis=1)
    packed, across = lax.optimization_barrier((packed, across))
    across = lax.all_gather(across, "row", axis=0)

    tall = spread_out(packed, "row", rows_n).reshape(rows_n * block, quarters * own).T
    strip = jnp.concatenate([tall[q * own : (q + 1) * own] for q in range(quarters)], axis=1)
    strip = jnp.concatenate([strip[:block], strip[block:, NB:]], axis=1)
    own_pieces = spread_out(strip, "col", chips, same_core)
    panel = covariance[:, :own].T.reshape(2, block, local_rows)
    own_pieces, panel = lax.optimization_barrier((own_pieces, panel))
    other_pieces = swap(own_pieces)
    own_panel = spread_out(panel, "col", chips, same_core)
    w0, w1, state = first_steps(at, own_pieces, other_pieces)
    state, own_panel, across = lax.optimization_barrier((state, own_panel, across))
    other_panel = swap(own_panel)
    w2 = last_step(state)
    return update_part(at, w0, w1, w2, own_panel, other_panel, across, covariance, fields)


def solution(mesh):
    return jax.shard_map(
        shards,
        mesh=mesh,
        in_specs=(P("row", "col"), P("col", "row")),
        out_specs=(P("row", "col"), P("col", "row")),
        check_vma=False,
    )
```
